32 devices in a mesh: pair: 8 (over z, y), row: 4 (over x, core).
Axes of the slice: x: 2, y: 2, z: 4, core: 2. Of those that a mesh axis runs over, the one named last changes fastest.
Arguments:
- snapshots: float32 [1024, 16384], P('pair', 'row'), may hold values from -50 to 50
- live_rows: int32 [4], P('row'), may hold values from 2048 to 4096, as said below
Outputs:
- rotated: float32 [1024, 16384], P('pair', 'row')
The draws below stay inside these ranges and needn't reach their ends.
Inputs may be any that keep to these rules, and one draw needn't show every extreme that they name: Row slot s of row index r is live when s < live_rows[r]; every draw has a row index with all 4096 slots live.
All inputs are finite; a program needn't handle non-finite values.
Results may differ from the reference program's by a relative error of at most 0.0003.
Values sent between devices are 32-bit elements; how exact they have to be, the bound alone decides.
A program may use at most 64 MiB of HBM per device.

```python
import math
import jax
import jax.numpy as jnp
from jax import lax

ROWS_DEV = 4096
BLOCK = 64
ROUNDS = 4
NS_STEPS = 3
ROWS = 16384
COLS = 1024
N_PAIR = 8
N_ROW = 4


def draw_snapshots(key, part):
    key_list = jax.random.split(jax.random.fold_in(key, 3), 3)
    column_scale = jnp.exp(jax.random.uniform(key_list[0], (COLS, 1), jnp.float32, math.log(0.3), math.log(3.0)))
    row_scale = jnp.exp(jax.random.uniform(key_list[1], (1, ROWS), jnp.float32, math.log(0.3), math.log(3.0)))
    base = jnp.clip(jax.random.normal(key_list[2], (COLS, ROWS), jnp.float32), -4.0, 4.0)
    return base * column_scale * row_scale


def draw_live_rows(key, part):
    first_key, second_key = jax.random.split(jax.random.fold_in(key, 7))
    counts = jax.random.randint(first_key, (N_ROW,), ROWS_DEV // 2, ROWS_DEV + 1)
    full_index = jax.random.randint(second_key, (), 0, N_ROW)
    return jnp.where(jnp.arange(N_ROW) == full_index, ROWS_DEV, counts).astype(jnp.int32)


def setup_inputs(seed: int = 0) -> dict:
    arg_keys = jax.random.split(jax.random.key(seed), 3)
    snapshots = draw_snapshots(jax.random.fold_in(arg_keys[2], 71), 0)
    live_rows = draw_live_rows(jax.random.fold_in(arg_keys[2], 71), 0)
    return {"snapshots": snapshots, "live_rows": live_rows}


EPSILON = 1e-06
PRECISE = lax.Precision.HIGHEST

def make_rotation(cross_block, column_norms):
    block_width = cross_block.shape[0]
    upper_norm = column_norms[:block_width][:, None]
    lower_norm = column_norms[block_width:][None, :]
    spread = lower_norm - upper_norm
    coupling = cross_block * spread / (spread * spread + 4.0 * cross_block * cross_block + upper_norm * lower_norm + EPSILON)
    blank_block = jnp.zeros((block_width, block_width), jnp.float32)
    generator = jnp.concatenate([jnp.concatenate([blank_block, coupling], 1), jnp.concatenate([-coupling.T, blank_block], 1)], 0)
    damping = 1.0 / jnp.sqrt(1.0 + 2.0 * jnp.sum(coupling * coupling))
    rotation = (jnp.eye(2 * block_width, dtype=jnp.float32) + generator) * damping
    for iteration in range(NS_STEPS):
        product = jnp.dot(rotation.T, rotation, precision=PRECISE, preferred_element_type=jnp.float32)
        rotation = 1.5 * rotation - 0.5 * jnp.dot(rotation, product, precision=PRECISE, preferred_element_type=jnp.float32)
    return rotation

def pair_round(pair_block):
    gram_matrix = jnp.dot(pair_block, pair_block.T, precision=PRECISE, preferred_element_type=jnp.float32)
    rotation = make_rotation(gram_matrix[:BLOCK, BLOCK:], jnp.diagonal(gram_matrix))
    return jnp.dot(rotation.T, pair_block, precision=PRECISE, preferred_element_type=jnp.float32)

def reference(snapshots, live_rows):
    slot_index = jnp.arange(ROWS, dtype=jnp.int32)
    live_limit = jnp.repeat(live_rows, ROWS_DEV)
    masked = jnp.where((slot_index % ROWS_DEV < live_limit)[None, :], snapshots, jnp.zeros((), jnp.float32))
    pair_rows = masked.reshape(N_PAIR, 2 * BLOCK, ROWS)
    for round_index in range(ROUNDS):
        pair_rows = lax.map(pair_round, pair_rows)
        if round_index + 1 < ROUNDS:
            top_blocks = pair_rows[:, :BLOCK]
            bottom_blocks = pair_rows[:, BLOCK:]
            new_tops = jnp.concatenate([top_blocks[:1], bottom_blocks[:1], top_blocks[1:N_PAIR - 1]], 0)
            new_bottoms = jnp.concatenate([bottom_blocks[1:], top_blocks[N_PAIR - 1:]], 0)
            pair_rows = jnp.concatenate([new_tops, new_bottoms], 1)
    return pair_rows.reshape(2 * BLOCK * N_PAIR, ROWS)
```

```python
import functools

import jax
import jax.numpy as jnp
from jax import lax
from jax.experimental import pallas as pl
from jax.experimental.pallas import tpu as pltpu
from jax.sharding import PartitionSpec as P

ROUNDS = 4
NS_STEPS = 3
EPSILON = 1e-06
PRECISE = lax.Precision.HIGHEST
MESH = pl.DeviceIdType.MESH
CHUNKS = 4


def nt(left, right):
    return lax.dot_general(
        left,
        right,
        (((1,), (1,)), ((), ())),
        precision=PRECISE,
        preferred_element_type=jnp.float32,
    )


def nn(left, right):
    return jnp.dot(left, right, precision=PRECISE, preferred_element_type=jnp.float32)


def eye_mask(rows, columns):
    row = lax.broadcasted_iota(jnp.int32, (rows, columns), 0)
    column = lax.broadcasted_iota(jnp.int32, (rows, columns), 1)
    return row == column


def pack(grams, width):
    full = 2 * width
    lane = lax.broadcasted_iota(jnp.int32, (width, full), 1)
    line = lax.broadcasted_iota(jnp.int32, (8, full), 0)
    diagonal = eye_mask(full, full)
    norms = [jnp.sum(jnp.where(diagonal, g, 0.0), axis=0, keepdims=True) for g in grams]
    cross = grams[0][:width]
    tail = jnp.where(line == 0, norms[0], 0.0)
    if len(grams) == 2:
        cross = jnp.where(lane < width, pltpu.roll(grams[1][:width], width, 1), cross)
        tail = jnp.where(line == 1, norms[1], tail)
    return cross, tail


def rotation_transposed(cross, norms, width):
    full = 2 * width
    lane = lax.broadcasted_iota(jnp.int32, (width, full), 1)
    cross = jnp.where(lane >= width, cross, 0.0)
    upper = jnp.sum(jnp.where(eye_mask(width, full), norms, 0.0), axis=1, keepdims=True)
    spread = norms - upper
    coupling = cross * spread / (spread * spread + 4.0 * cross * cross + upper * norms + EPSILON)
    squares = jnp.sum(jnp.sum(coupling * coupling, axis=1, keepdims=True), axis=0, keepdims=True)
    damping = 1.0 / jnp.sqrt(1.0 + 2.0 * squares)
    corner = jnp.concatenate([coupling, jnp.zeros((width, full), jnp.float32)], 0)
    identity = jnp.where(eye_mask(full, full), 1.0, 0.0)
    return (identity - corner + corner.T) * damping


def orthogonalised(turns):
    for _ in range(NS_STEPS):
        products = [nt(t, t) for t in turns]
        turns = [1.5 * t - 0.5 * nn(g, t) for t, g in zip(turns, products)]
    return turns


def kernel(
    pairs, rows, live_ref, x_ref, out_ref, sent0, held1, sent1, held2, sent2, held3, grams,
    gram_send, gram_recv, send1, recv1, send2, recv2, send3, recv3,
):
    p, r = lax.axis_index("pair"), lax.axis_index("row")
    plane, y = p // 2, p % 2
    last_plane = pairs // 2 - 1
    width = x_ref.shape[0] // 2
    cells = x_ref.shape[1]
    half = cells // 2
    step = half // CHUNKS
    first, last = plane == 0, plane == last_plane

    barrier = pltpu.get_barrier_semaphore()
    for k in range(1, 2 * rows):
        other = lax.rem(y * rows + r + k, 2 * rows)
        pl.semaphore_signal(
            barrier, inc=1, device_id=(2 * plane + other // rows, lax.rem(other, rows)), device_id_type=MESH
        )
    for side in range(2):
        @pl.when(plane > 0)
        def _():
            pl.semaphore_signal(barrier, inc=1, device_id=(2 * plane - 2 + side, r), device_id_type=MESH)

        @pl.when(plane < last_plane)
        def _():
            pl.semaphore_signal(barrier, inc=1, device_id=(2 * plane + 2 + side, r), device_id_type=MESH)
    near = jnp.where(plane > 0, 2, 0) + jnp.where(plane < last_plane, 2, 0)
    pl.semaphore_wait(barrier, 2 * rows - 1 + near)

    def columns(h, c):
        return pl.ds(h * half + c * step, step)

    def summed(round_index, gram_list):
        cross, tail = pack(gram_list, width)
        plane_wide = len(gram_list) == 2
        count = 2 * rows if plane_wide else rows
        me = y * rows + r if plane_wide else r
        grams[round_index, me, pl.ds(0, width)] = cross
        grams[round_index, me, pl.ds(width, 8)] = tail
        copies = []
        for k in range(1, count):
            other = lax.rem(me + k, count)
            target = (2 * plane + other // rows, lax.rem(other, rows)) if plane_wide else (p, other)
            copy = pltpu.make_async_remote_copy(
                src_ref=grams.at[round_index, me],
                dst_ref=grams.at[round_index, me],
                send_sem=gram_send.at[round_index, k],
                recv_sem=gram_recv.at[round_index, k],
                device_id=target,
                device_id_type=MESH,
            )
            copy.start()
            copies.append(copy)
        for copy in copies:
            copy.wait()
        total = grams[round_index, 0]
        for k in range(1, count):
            total = total + grams[round_index, k]
        turns = [rotation_transposed(total[:width], total[width : width + 1], width)]
        if plane_wide:
            turns.append(
                rotation_transposed(pltpu.roll(total[:width], width, 1), total[width + 1 : width + 2], width)
            )
        return orthogonalised(turns)

    def goes_to(pair, side):
        if side == 0:
            pair_to = jnp.where(pair == 0, 0, jnp.where(pair == pairs - 1, pairs - 1, pair + 1))
            side_to = jnp.where(pair == pairs - 1, 1, 0)
        else:
            pair_to = jnp.where(pair == 0, 1, pair - 1)
            side_to = jnp.where(pair == 0, 0, 1)
        return pair_to, side_to

    came_from = [
        jnp.where(first, 0, 2 * plane - 1),
        2 * plane + 1,
        2 * plane,
        jnp.where(last, 2 * plane + 1, 2 * plane + 2),
    ]

    def start(local, source, target, send_sem, recv_sem, pair_to):
        @pl.when(local)
        def _():
            pltpu.make_async_copy(source, target, recv_sem).start()

        @pl.when(jnp.logical_not(local))
        def _():
            remote(source, target, send_sem, recv_sem, pair_to).start()

    def remote(source, target, send_sem, recv_sem, pair_to):
        return pltpu.make_async_remote_copy(
            src_ref=source,
            dst_ref=target,
            send_sem=send_sem,
            recv_sem=recv_sem,
            device_id=(pair_to, r),
            device_id_type=MESH,
        )

    def wait_arrival(source, target, recv_sem):
        pltpu.make_async_copy(source, target, recv_sem).wait()

    def wait_sent(local, source, target, send_sem, recv_sem, pair_to):
        @pl.when(jnp.logical_not(local))
        def _():
            remote(source, target, send_sem, recv_sem, pair_to).wait_send()

    live = live_ref[0]

    def masked(h, c):
        slot = lax.broadcasted_iota(jnp.int32, (1, step), 1) + (h * half + c * step)
        return jnp.where(slot < live, x_ref[:, columns(h, c)], 0.0)

    gram = jnp.zeros((2 * width, 2 * width), jnp.float32)
    for h in range(2):
        for c in range(CHUNKS):
            block = masked(h, c)
            gram = gram + nt(block, block)
    (turn,) = summed(0, [gram])

    def move1(side, h, c):
        pair_to, side_to = goes_to(p, side)
        slot = 2 * lax.rem(pair_to, 2) + side_to
        device = 2 * (pair_to // 2) + h
        part = pl.ds(c * step, step)
        return (
            device == p,
            sent0.at[h, side, :, part],
            held1.at[slot, :, part],
            send1.at[side, h, c],
            recv1.at[slot, c],
            device,
        )

    for c in range(CHUNKS):
        for h in range(2):
            result = nn(turn, masked(h, c))
            sent0[h, :, :, pl.ds(c * step, step)] = result.reshape(2, width, step)
            for side in range(2):
                start(*move1(side, h, c))

    def plane_round(round_index, held, recv):
        gram_list = [jnp.zeros((2 * width, 2 * width), jnp.float32)] * 2
        for c in range(CHUNKS):
            part = pl.ds(c * step, step)
            for slot in range(4):
                wait_arrival(held.at[slot, :, part], held.at[slot, :, part], recv.at[slot, c])
            for which in range(2):
                block = held[2 * which : 2 * which + 2, :, part].reshape(2 * width, step)
                gram_list[which] = gram_list[which] + nt(block, block)
        return summed(round_index, gram_list)

    def rotated(turns, held, sent, c):
        part = pl.ds(c * step, step)
        for which in range(2):
            block = held[2 * which : 2 * which + 2, :, part].reshape(2 * width, step)
            sent[2 * which : 2 * which + 2, :, part] = nn(turns[which], block).reshape(2, width, step)

    def move2(pair_side, c):
        which, side = pair_side // 2, pair_side % 2
        pair_to, side_to = goes_to(2 * plane + which, side)
        slot = 2 * lax.rem(pair_to, 2) + side_to
        device = 2 * (pair_to // 2) + y
        part = pl.ds(c * step, step)
        return (
            device == p,
            sent1.at[pair_side, :, part],
            held2.at[slot, :, part],
            send2.at[pair_side, c],
            recv2.at[slot, c],
            device,
        )

    def move3(pair_side, c):
        which, side = pair_side // 2, pair_side % 2
        pair_to, side_to = goes_to(2 * plane + which, side)
        part = pl.ds(c * step, step)
        return (
            pair_to == p,
            sent2.at[pair_side, :, part],
            held3.at[y, side_to, :, part],
            send3.at[pair_side, c],
            recv3.at[y, side_to, c],
            pair_to,
        )

    turns = plane_round(1, held1, recv1)
    for c in range(CHUNKS):
        rotated(turns, held1, sent1, c)
        for pair_side in range(4):
            start(*move2(pair_side, c))
    turns = plane_round(2, held2, recv2)
    for c in range(CHUNKS):
        rotated(turns, held2, sent2, c)
        for pair_side in range(4):
            start(*move3(pair_side, c))

    gram = jnp.zeros((2 * width, 2 * width), jnp.float32)
    for c in range(CHUNKS):
        part = pl.ds(c * step, step)
        for h in range(2):
            for side in range(2):
                ref = held3.at[h, side, :, part]
                wait_arrival(ref, ref, recv3.at[h, side, c])
            block = held3[h, :, :, part].reshape(2 * width, step)
            gram = gram + nt(block, block)
    (turn,) = summed(3, [gram])
    for h in range(2):
        for c in range(CHUNKS):
            block = held3[h, :, :, pl.ds(c * step, step)].reshape(2 * width, step)
            out_ref[:, columns(h, c)] = nn(turn, block)

    for c in range(CHUNKS):
        for side in range(2):
            for h in range(2):
                wait_sent(*move1(side, h, c))
        for pair_side in range(4):
            wait_sent(*move2(pair_side, c))
            wait_sent(*move3(pair_side, c))


def solution(mesh):
    pairs, rows = mesh.shape["pair"], mesh.shape["row"]

    def body(snapshots, live_rows):
        full, cells = snapshots.shape
        width, half = full // 2, cells // 2
        state = pltpu.VMEM((4, width, half), jnp.float32)
        stated = pltpu.VMEM((2, 2, width, half), jnp.float32)
        return pl.pallas_call(
            functools.partial(kernel, pairs, rows),
            out_shape=jax.ShapeDtypeStruct(snapshots.shape, jnp.float32),
            in_specs=[
                pl.BlockSpec(memory_space=pltpu.SMEM),
                pl.BlockSpec(memory_space=pltpu.VMEM),
            ],
            out_specs=pl.BlockSpec(memory_space=pltpu.VMEM),
            scratch_shapes=[
                stated,
                state,
                state,
                state,
                state,
                stated,
                pltpu.VMEM((ROUNDS, 2 * rows, width + 8, full), jnp.float32),
                pltpu.SemaphoreType.DMA((ROUNDS, 2 * rows)),
                pltpu.SemaphoreType.DMA((ROUNDS, 2 * rows)),
                pltpu.SemaphoreType.DMA((2, 2, CHUNKS)),
                pltpu.SemaphoreType.DMA((4, CHUNKS)),
                pltpu.SemaphoreType.DMA((4, CHUNKS)),
                pltpu.SemaphoreType.DMA((4, CHUNKS)),
                pltpu.SemaphoreType.DMA((4, CHUNKS)),
                pltpu.SemaphoreType.DMA((2, 2, CHUNKS)),
            ],
            compiler_params=pltpu.CompilerParams(
                collective_id=0, has_side_effects=True, vmem_limit_bytes=48 * 1024 * 1024
            ),
        )(live_rows, snapshots)

    return jax.shard_map(
        body,
        mesh=mesh,
        in_specs=(P("pair", "row"), P("row")),
        out_specs=P("pair", "row"),
        check_vma=False,
    )
```

```python
import functools

import jax
import jax.numpy as jnp
from jax import lax
from jax.experimental import pallas as pl
from jax.experimental.pallas import tpu as pltpu
from jax.sharding import PartitionSpec as P

ROUNDS = 4
NS_STEPS = 3
EPSILON = 1e-06
PRECISE = lax.Precision.HIGHEST
MESH = pl.DeviceIdType.MESH
CHUNKS = 4
EARLY = 1
LATE = 1


def nt(left, right):
    return lax.dot_general(
        left,
        right,
        (((1,), (1,)), ((), ())),
        precision=PRECISE,
        preferred_element_type=jnp.float32,
    )


def nn(left, right):
    return jnp.dot(left, right, precision=PRECISE, preferred_element_type=jnp.float32)


def eye_mask(rows, columns):
    row = lax.broadcasted_iota(jnp.int32, (rows, columns), 0)
    column = lax.broadcasted_iota(jnp.int32, (rows, columns), 1)
    return row == column


def halves(block):
    high = block.astype(jnp.bfloat16)
    return high, (block - high.astype(jnp.float32)).astype(jnp.bfloat16)


def gram_parts(block):
    high, low = halves(block)
    return lax.dot_general(
        high,
        jnp.concatenate([high, low], 0),
        (((1,), (1,)), ((), ())),
        preferred_element_type=jnp.float32,
    )


def gram_of(parts):
    full = parts.shape[0]
    mixed = parts[:, full:]
    return parts[:, :full] + mixed + mixed.T


def turn_halves(turn):
    high, low = halves(turn)
    return jnp.concatenate([high, high], 1), low


def turned(turn, block):
    wide, low_turn = turn
    high, low = halves(block)
    return jnp.dot(
        wide, jnp.concatenate([high, low], 0), preferred_element_type=jnp.float32
    ) + jnp.dot(low_turn, high, preferred_element_type=jnp.float32)


def norms_of(gram):
    return jnp.sum(jnp.where(eye_mask(*gram.shape), gram, 0.0), axis=0, keepdims=True)


def pack_two(first, second, width):
    lane = lax.broadcasted_iota(jnp.int32, (width, 2 * width), 1)
    line = lax.broadcasted_iota(jnp.int32, (8, 2 * width), 0)
    cross = jnp.where(lane < width, pltpu.roll(second[:width], width, 1), first[:width])
    return cross, jnp.where(line == 0, norms_of(first), norms_of(second))


def pack_one(gram, width):
    part = width // 2
    lane = lax.broadcasted_iota(jnp.int32, (part, 2 * width), 1)
    cross = jnp.where(lane < width, pltpu.roll(gram[:part], width, 1), gram[part:width])
    return cross, jnp.broadcast_to(norms_of(gram), (8, 2 * width))


def rotation_transposed(cross, norms, width):
    full = 2 * width
    lane = lax.broadcasted_iota(jnp.int32, (width, full), 1)
    cross = jnp.where(lane >= width, cross, 0.0)
    upper = jnp.sum(jnp.where(eye_mask(width, full), norms, 0.0), axis=1, keepdims=True)
    spread = norms - upper
    coupling = cross * spread / (spread * spread + 4.0 * cross * cross + upper * norms + EPSILON)
    squares = jnp.sum(jnp.sum(coupling * coupling, axis=1, keepdims=True), axis=0, keepdims=True)
    damping = 1.0 / jnp.sqrt(1.0 + 2.0 * squares)
    corner = jnp.concatenate([coupling, jnp.zeros((width, full), jnp.float32)], 0)
    identity = jnp.where(eye_mask(full, full), 1.0, 0.0)
    return (identity - corner + corner.T) * damping


def orthogonalised(turns):
    for _ in range(NS_STEPS):
        products = [nt(t, t) for t in turns]
        turns = [1.5 * t - 0.5 * nn(g, t) for t, g in zip(turns, products)]
    return turns


def kernel(
    pairs, rows, live_ref, x_hbm, out_ref, x_ref, raw, sent0, held1, sent1, held2, sent2, held3, final,
    turn_out, turn_in, singles, doubles, load_sem, raw_send, raw_recv, turn_sem,
    one_send, one_recv, two_send, two_recv, move_send, move_recv, last_send, last_recv,
):
    p, r = lax.axis_index("pair"), lax.axis_index("row")
    plane, y = p // 2, p % 2
    last_plane = pairs // 2 - 1
    partner = 2 * plane + 1 - y
    full, cells = x_ref.shape
    width = full // 2
    half = cells // 2
    step = half // CHUNKS
    first, last = plane == 0, plane == last_plane

    def columns(h, c):
        return pl.ds(pl.multiple_of(h * half + c * step, step), step)

    def load(k):
        part = pl.ds(k * step, step)
        return pltpu.make_async_copy(x_hbm.at[:, part], x_ref.at[:, part], load_sem.at[k])

    for k in range(2 * CHUNKS):
        load(k).start()

    barrier = pltpu.get_barrier_semaphore()
    for k in range(1, 2 * rows):
        other = lax.rem(y * rows + r + k, 2 * rows)
        pl.semaphore_signal(
            barrier, inc=1, device_id=(2 * plane + other // rows, lax.rem(other, rows)), device_id_type=MESH
        )

    @pl.when(plane > 0)
    def _():
        pl.semaphore_signal(barrier, inc=1, device_id=(p - 2, r), device_id_type=MESH)

    @pl.when(plane < last_plane)
    def _():
        pl.semaphore_signal(barrier, inc=1, device_id=(p + 2, r), device_id_type=MESH)

    near = jnp.where(plane > 0, 1, 0) + jnp.where(plane < last_plane, 1, 0)
    pl.semaphore_wait(barrier, 2 * rows - 1 + near)

    def remote(source, target, send_sem, recv_sem, pair_to, row_to=r):
        return pltpu.make_async_remote_copy(
            src_ref=source,
            dst_ref=target,
            send_sem=send_sem,
            recv_sem=recv_sem,
            device_id=(pair_to, row_to),
            device_id_type=MESH,
        )

    def arrived(target, recv_sem):
        pltpu.make_async_copy(target, target, recv_sem).wait()

    def raw_copy(c):
        return remote(
            x_hbm.at[:, columns(1 - y, c)], raw.at[:, pl.ds(c * step, step)], raw_send.at[c], raw_recv.at[c], partner
        )

    def share(buffer, slot, me, count, send_sem, recv_sem, target):
        copies = []
        for k in range(1, count):
            other = lax.rem(me + k, count)
            copy = remote(
                buffer.at[slot, me], buffer.at[slot, me], send_sem.at[slot, k], recv_sem.at[slot, k], *target(other)
            )
            copy.start()
            copies.append(copy)
        return copies

    def total(buffer, slot, count, copies):
        for copy in copies:
            copy.wait()
        result = buffer[slot, 0]
        for k in range(1, count):
            result = result + buffer[slot, k]
        return result

    def share_one(slot, gram):
        cross, tail = pack_one(gram, width)
        singles[slot, r, pl.ds(0, width // 2)] = cross
        singles[slot, r, pl.ds(width // 2, 8)] = tail
        return share(singles, slot, r, rows, one_send, one_recv, lambda other: (p, other))

    def turn_one(slot, copies):
        part = width // 2
        result = total(singles, slot, rows, copies)
        cross = jnp.concatenate([pltpu.roll(result[:part], width, 1), result[:part]], 0)
        return orthogonalised([rotation_transposed(cross, result[part : part + 1], width)])[0]

    def turn_two(slot, grams):
        cross, tail = pack_two(grams[0], grams[1], width)
        me = y * rows + r
        doubles[slot, me, pl.ds(0, width)] = cross
        doubles[slot, me, pl.ds(width, 8)] = tail
        copies = share(
            doubles, slot, me, 2 * rows, two_send, two_recv,
            lambda other: (2 * plane + other // rows, lax.rem(other, rows)),
        )
        result = total(doubles, slot, 2 * rows, copies)
        return orthogonalised([
            rotation_transposed(result[:width], result[width : width + 1], width),
            rotation_transposed(pltpu.roll(result[:width], width, 1), result[width + 1 : width + 2], width),
        ])

    def goes_to(pair, side):
        if side == 0:
            pair_to = jnp.where(pair == 0, 0, jnp.where(pair == pairs - 1, pairs - 1, pair + 1))
            side_to = jnp.where(pair == pairs - 1, 1, 0)
        else:
            pair_to = jnp.where(pair == 0, 1, pair - 1)
            side_to = jnp.where(pair == 0, 0, 1)
        return pair_to, side_to

    def move(number, sent, held, which, side, c):
        pair_to, side_to = goes_to(2 * plane + which, side)
        slot = 2 * lax.rem(pair_to, 2) + side_to
        device = 2 * (pair_to // 2) + y
        part = pl.ds(c * step, step)
        source = sent.at[2 * which + side, :, part]
        target = held.at[slot, :, part]
        recv_sem = move_recv.at[number, slot, c]
        copy = remote(source, target, move_send.at[number, 2 * which + side, c], recv_sem, device)
        return device == p, copy, pltpu.make_async_copy(source, target, recv_sem)

    def start_move(*place):
        local, copy, inside = move(*place)

        @pl.when(local)
        def _():
            inside.start()

        @pl.when(jnp.logical_not(local))
        def _():
            copy.start()

    def end_move(*place):
        local, copy, _ = move(*place)

        @pl.when(jnp.logical_not(local))
        def _():
            copy.wait_send()

    def wait_slots(number, held, slots, c):
        for slot in slots:
            arrived(held.at[slot, :, pl.ds(c * step, step)], move_recv.at[number, slot, c])

    def pair_block(held, which, c):
        return held[pl.ds(2 * which, 2), :, pl.ds(c * step, step)].reshape(full, step)

    live = live_ref[0]

    def masked(block, h, c):
        slot = lax.broadcasted_iota(jnp.int32, (1, step), 1) + (h * half + c * step)
        return jnp.where(slot < live, block, 0.0)

    for c in range(EARLY):
        raw_copy(c).start()
    parts = jnp.zeros((full, 2 * full), jnp.float32)
    for k in range(2 * CHUNKS):
        load(k).wait()
        h, c = k // CHUNKS, k % CHUNKS
        parts = parts + gram_parts(masked(x_ref[:, columns(h, c)], h, c))
    copies = share_one(0, gram_of(parts))
    for c in range(EARLY, CHUNKS - 1):
        raw_copy(c).start()
    turn = turn_one(0, copies)
    turn_out[...] = turn
    turn_copy = remote(turn_out, turn_in, turn_sem.at[0], turn_sem.at[1], partner)
    turn_copy.start()
    for c in range(max(EARLY, CHUNKS - 1), CHUNKS):
        raw_copy(c).start()

    def first_turn(which, turn_parts, block, c):
        sent0[pl.ds(2 * which, 2), :, pl.ds(c * step, step)] = turned(turn_parts, masked(block, y, c)).reshape(
            2, width, step
        )
        for side in range(2):
            for number in range(2):
                @pl.when(which == number)
                def _():
                    start_move(0, sent0, held1, number, side, c)

    own = turn_halves(turn)
    for c in range(CHUNKS):
        first_turn(y, own, x_ref[:, columns(y, c)], c)
    turn_copy.wait()
    other = turn_halves(turn_in[...])
    for c in range(CHUNKS):
        raw_copy(c).wait_recv()
        first_turn(1 - y, other, raw[:, pl.ds(c * step, step)], c)

    def plane_gram(number, held):
        parts = [jnp.zeros((full, 2 * full), jnp.float32)] * 2
        for c in range(CHUNKS):
            wait_slots(number, held, range(4), c)
            parts = [parts[which] + gram_parts(pair_block(held, which, c)) for which in range(2)]
        return [gram_of(part) for part in parts]

    for number, held, sent, held_next in ((0, held1, sent1, held2), (1, held2, sent2, held3)):
        turns = [turn_halves(t) for t in turn_two(number, plane_gram(number, held))]
        for c in range(CHUNKS):
            for which in range(2):
                sent[2 * which : 2 * which + 2, :, pl.ds(c * step, step)] = turned(
                    turns[which], pair_block(held, which, c)
                ).reshape(2, width, step)
                for side in range(2):
                    start_move(number + 1, sent, held_next, which, side, c)

    def hand_back(side, c):
        part = pl.ds(c * step, step)
        return remote(
            held3.at[2 * (1 - y) + side, :, part],
            final.at[side, :, part],
            last_send.at[side, c],
            last_recv.at[side, c],
            partner,
        )

    for c in range(CHUNKS):
        wait_slots(2, held3, (1, 2), c)
        for number in range(2):
            @pl.when(y == number)
            def _():
                hand_back(number, c).start()
    parts = [jnp.zeros((full, 2 * full), jnp.float32)] * 2
    for c in range(CHUNKS):
        wait_slots(2, held3, (0, 3), c)
        if c < LATE:
            for number in range(2):
                @pl.when(y == number)
                def _():
                    hand_back(1 - number, c).start()
        parts = [parts[which] + gram_parts(pair_block(held3, which, c)) for which in range(2)]
    mine, theirs = (jnp.where(y == k, gram_of(parts[0]), gram_of(parts[1])) for k in range(2))
    cross, tail = pack_one(theirs, width)
    singles[2, 0, pl.ds(0, width // 2)] = cross
    singles[2, 0, pl.ds(width // 2, 8)] = tail
    swap = remote(singles.at[2, 0], singles.at[2, 1], turn_sem.at[2], turn_sem.at[3], partner)
    swap.start()
    for c in range(LATE, CHUNKS):
        for number in range(2):
            @pl.when(y == number)
            def _():
                hand_back(1 - number, c).start()
    cross, tail = pack_one(mine, width)
    swap.wait()
    singles[1, r, pl.ds(0, width // 2)] = cross + singles[2, 1, pl.ds(0, width // 2)]
    singles[1, r, pl.ds(width // 2, 8)] = tail + singles[2, 1, pl.ds(width // 2, 8)]
    copies = share(singles, 1, r, rows, one_send, one_recv, lambda other: (p, other))
    own = turn_halves(turn_one(1, copies))
    for c in range(CHUNKS):
        out_ref[:, columns(y, c)] = turned(own, pair_block(held3, y, c))
    for c in range(CHUNKS):
        for side in range(2):
            hand_back(side, c).wait_recv()
        out_ref[:, columns(1 - y, c)] = turned(own, final[:, :, pl.ds(c * step, step)].reshape(full, step))

    for c in range(CHUNKS):
        raw_copy(c).wait_send()
        for which in range(2):
            for side in range(2):
                for number, sent, held in ((0, sent0, held1), (1, sent1, held2), (2, sent2, held3)):
                    end_move(number, sent, held, which, side, c)
        for side in range(2):
            hand_back(side, c).wait_send()


def solution(mesh):
    pairs, rows = mesh.shape["pair"], mesh.shape["row"]

    def body(snapshots, live_rows):
        full, cells = snapshots.shape
        width, half = full // 2, cells // 2
        state = pltpu.VMEM((4, width, half), jnp.float32)
        copies = pltpu.SemaphoreType.DMA
        return pl.pallas_call(
            functools.partial(kernel, pairs, rows),
            out_shape=jax.ShapeDtypeStruct(snapshots.shape, jnp.float32),
            in_specs=[
                pl.BlockSpec(memory_space=pltpu.SMEM),
                pl.BlockSpec(memory_space=pltpu.HBM),
            ],
            out_specs=pl.BlockSpec(memory_space=pltpu.VMEM),
            scratch_shapes=[
                pltpu.VMEM((full, cells), jnp.float32),
                pltpu.VMEM((full, half), jnp.float32),
                state,
                state,
                state,
                state,
                state,
                state,
                pltpu.VMEM((2, width, half), jnp.float32),
                pltpu.VMEM((full, full), jnp.float32),
                pltpu.VMEM((full, full), jnp.float32),
                pltpu.VMEM((3, max(rows, 2), width // 2 + 8, full), jnp.float32),
                pltpu.VMEM((2, 2 * rows, width + 8, full), jnp.float32),
                copies((2 * CHUNKS,)),
                copies((CHUNKS,)),
                copies((CHUNKS,)),
                copies((4,)),
                copies((2, rows)),
                copies((2, rows)),
                copies((2, 2 * rows)),
                copies((2, 2 * rows)),
                copies((3, 4, CHUNKS)),
                copies((3, 4, CHUNKS)),
                copies((2, CHUNKS)),
                copies((2, CHUNKS)),
            ],
            compiler_params=pltpu.CompilerParams(
                collective_id=0, has_side_effects=True, vmem_limit_bytes=48 * 1024 * 1024
            ),
        )(live_rows, snapshots)

    return jax.shard_map(
        body,
        mesh=mesh,
        in_specs=(P("pair", "row"), P("row")),
        out_specs=P("pair", "row"),
        check_vma=False,
    )
```

```python
import functools

import jax
import jax.numpy as jnp
from jax import lax
from jax.experimental import pallas as pl
from jax.experimental.pallas import tpu as pltpu
from jax.sharding import PartitionSpec as P

ROUNDS = 4
NS_STEPS = 3
EPSILON = 1e-06
MESH = pl.DeviceIdType.MESH
CHUNKS = 4
EARLY = 1
LATE = 1


def own_product(block):
    high, low = halves(block)
    dims = (((1,), (1,)), ((), ()))
    return lax.dot_general(
        jnp.concatenate([high, high], 1),
        jnp.concatenate([high, low], 1),
        dims,
        preferred_element_type=jnp.float32,
    ) + lax.dot_general(low, high, dims, preferred_element_type=jnp.float32)


def eye_mask(rows, columns):
    row = lax.broadcasted_iota(jnp.int32, (rows, columns), 0)
    column = lax.broadcasted_iota(jnp.int32, (rows, columns), 1)
    return row == column


def halves(block):
    high = block.astype(jnp.bfloat16)
    return high, (block - high.astype(jnp.float32)).astype(jnp.bfloat16)


def gram_parts(block):
    high, low = halves(block)
    return lax.dot_general(
        high,
        jnp.concatenate([high, low], 0),
        (((1,), (1,)), ((), ())),
        preferred_element_type=jnp.float32,
    )


def gram_of(parts):
    full = parts.shape[0]
    mixed = parts[:, full:]
    return parts[:, :full] + mixed + mixed.T


def turn_halves(turn):
    high, low = halves(turn)
    return jnp.concatenate([high, high], 1), low


def turned(turn, block):
    wide, low_turn = turn
    high, low = halves(block)
    return jnp.dot(
        wide, jnp.concatenate([high, low], 0), preferred_element_type=jnp.float32
    ) + jnp.dot(low_turn, high, preferred_element_type=jnp.float32)


def norms_of(gram):
    return jnp.sum(jnp.where(eye_mask(*gram.shape), gram, 0.0), axis=0, keepdims=True)


def pack_two(first, second, width):
    lane = lax.broadcasted_iota(jnp.int32, (width, 2 * width), 1)
    line = lax.broadcasted_iota(jnp.int32, (8, 2 * width), 0)
    cross = jnp.where(lane < width, pltpu.roll(second[:width], width, 1), first[:width])
    return cross, jnp.where(line == 0, norms_of(first), norms_of(second))


def pack_one(gram, width):
    part = width // 2
    lane = lax.broadcasted_iota(jnp.int32, (part, 2 * width), 1)
    cross = jnp.where(lane < width, pltpu.roll(gram[:part], width, 1), gram[part:width])
    return cross, jnp.broadcast_to(norms_of(gram), (8, 2 * width))


def rotation_transposed(cross, norms, width):
    full = 2 * width
    lane = lax.broadcasted_iota(jnp.int32, (width, full), 1)
    cross = jnp.where(lane >= width, cross, 0.0)
    upper = jnp.sum(jnp.where(eye_mask(width, full), norms, 0.0), axis=1, keepdims=True)
    spread = norms - upper
    coupling = cross * spread / (spread * spread + 4.0 * cross * cross + upper * norms + EPSILON)
    squares = jnp.sum(jnp.sum(coupling * coupling, axis=1, keepdims=True), axis=0, keepdims=True)
    damping = 1.0 / jnp.sqrt(1.0 + 2.0 * squares)
    corner = jnp.concatenate([coupling, jnp.zeros((width, full), jnp.float32)], 0)
    identity = jnp.where(eye_mask(full, full), 1.0, 0.0)
    return (identity - corner + corner.T) * damping


def orthogonalised(turns):
    for _ in range(NS_STEPS):
        products = [own_product(t) for t in turns]
        turns = [1.5 * t - 0.5 * turned(turn_halves(g), t) for t, g in zip(turns, products)]
    return turns


def kernel(
    pairs, rows, live_ref, x_hbm, out_ref, x_ref, raw, sent0, held1, sent1, held2, sent2, held3, final,
    turn_out, turn_in, singles, doubles, load_sem, raw_send, raw_recv, turn_sem,
    one_send, one_recv, two_send, two_recv, move_send, move_recv, last_send, last_recv,
):
    p, r = lax.axis_index("pair"), lax.axis_index("row")
    plane, y = p // 2, p % 2
    last_plane = pairs // 2 - 1
    partner = 2 * plane + 1 - y
    full, cells = x_ref.shape
    width = full // 2
    half = cells // 2
    step = half // CHUNKS
    first, last = plane == 0, plane == last_plane

    def columns(h, c):
        return pl.ds(pl.multiple_of(h * half + c * step, step), step)

    def load(k):
        part = pl.ds(k * step, step)
        return pltpu.make_async_copy(x_hbm.at[:, part], x_ref.at[:, part], load_sem.at[k])

    for k in range(2 * CHUNKS):
        load(k).start()

    barrier = pltpu.get_barrier_semaphore()
    for k in range(1, 2 * rows):
        other = lax.rem(y * rows + r + k, 2 * rows)
        pl.semaphore_signal(
            barrier, inc=1, device_id=(2 * plane + other // rows, lax.rem(other, rows)), device_id_type=MESH
        )

    @pl.when(plane > 0)
    def _():
        pl.semaphore_signal(barrier, inc=1, device_id=(p - 2, r), device_id_type=MESH)

    @pl.when(plane < last_plane)
    def _():
        pl.semaphore_signal(barrier, inc=1, device_id=(p + 2, r), device_id_type=MESH)

    near = jnp.where(plane > 0, 1, 0) + jnp.where(plane < last_plane, 1, 0)
    pl.semaphore_wait(barrier, 2 * rows - 1 + near)

    def remote(source, target, send_sem, recv_sem, pair_to, row_to=r):
        return pltpu.make_async_remote_copy(
            src_ref=source,
            dst_ref=target,
            send_sem=send_sem,
            recv_sem=recv_sem,
            device_id=(pair_to, row_to),
            device_id_type=MESH,
        )

    def arrived(target, recv_sem):
        pltpu.make_async_copy(target, target, recv_sem).wait()

    def raw_copy(c):
        return remote(
            x_hbm.at[:, columns(1 - y, c)], raw.at[:, pl.ds(c * step, step)], raw_send.at[c], raw_recv.at[c], partner
        )

    def share(buffer, slot, me, count, send_sem, recv_sem, target):
        copies = []
        for k in range(1, count):
            other = lax.rem(me + k, count)
            copy = remote(
                buffer.at[slot, me], buffer.at[slot, me], send_sem.at[slot, k], recv_sem.at[slot, k], *target(other)
            )
            copy.start()
            copies.append(copy)
        return copies

    def total(buffer, slot, count, copies):
        for copy in copies:
            copy.wait()
        result = buffer[slot, 0]
        for k in range(1, count):
            result = result + buffer[slot, k]
        return result

    def share_one(slot, gram):
        cross, tail = pack_one(gram, width)
        singles[slot, r, pl.ds(0, width // 2)] = cross
        singles[slot, r, pl.ds(width // 2, 8)] = tail
        return share(singles, slot, r, rows, one_send, one_recv, lambda other: (p, other))

    def turn_one(slot, copies):
        part = width // 2
        result = total(singles, slot, rows, copies)
        cross = jnp.concatenate([pltpu.roll(result[:part], width, 1), result[:part]], 0)
        return orthogonalised([rotation_transposed(cross, result[part : part + 1], width)])[0]

    def turn_two(slot, grams):
        cross, tail = pack_two(grams[0], grams[1], width)
        me = y * rows + r
        doubles[slot, me, pl.ds(0, width)] = cross
        doubles[slot, me, pl.ds(width, 8)] = tail
        copies = share(
            doubles, slot, me, 2 * rows, two_send, two_recv,
            lambda other: (2 * plane + other // rows, lax.rem(other, rows)),
        )
        result = total(doubles, slot, 2 * rows, copies)
        return orthogonalised([
            rotation_transposed(result[:width], result[width : width + 1], width),
            rotation_transposed(pltpu.roll(result[:width], width, 1), result[width + 1 : width + 2], width),
        ])

    def goes_to(pair, side):
        if side == 0:
            pair_to = jnp.where(pair == 0, 0, jnp.where(pair == pairs - 1, pairs - 1, pair + 1))
            side_to = jnp.where(pair == pairs - 1, 1, 0)
        else:
            pair_to = jnp.where(pair == 0, 1, pair - 1)
            side_to = jnp.where(pair == 0, 0, 1)
        return pair_to, side_to

    def move(number, sent, held, which, side, c):
        pair_to, side_to = goes_to(2 * plane + which, side)
        slot = 2 * lax.rem(pair_to, 2) + side_to
        device = 2 * (pair_to // 2) + y
        part = pl.ds(c * step, step)
        source = sent.at[2 * which + side, :, part]
        target = held.at[slot, :, part]
        recv_sem = move_recv.at[number, slot, c]
        copy = remote(source, target, move_send.at[number, 2 * which + side, c], recv_sem, device)
        return device == p, copy, pltpu.make_async_copy(source, target, recv_sem)

    def start_move(*place):
        local, copy, inside = move(*place)
        if place[3] == place[4]:
            inside.start()
            return

        @pl.when(local)
        def _():
            inside.start()

        @pl.when(jnp.logical_not(local))
        def _():
            copy.start()

    def end_move(*place):
        if place[3] == place[4]:
            return
        local, copy, _ = move(*place)

        @pl.when(jnp.logical_not(local))
        def _():
            copy.wait_send()

    def wait_slots(number, held, slots, c):
        for slot in slots:
            arrived(held.at[slot, :, pl.ds(c * step, step)], move_recv.at[number, slot, c])

    def pair_block(held, which, c):
        return held[pl.ds(2 * which, 2), :, pl.ds(c * step, step)].reshape(full, step)

    live = live_ref[0]

    def masked(block, h, c):
        slot = lax.broadcasted_iota(jnp.int32, (1, step), 1) + (h * half + c * step)
        return jnp.where(slot < live, block, 0.0)

    for c in range(EARLY):
        raw_copy(c).start()
    parts = jnp.zeros((full, 2 * full), jnp.float32)
    for k in range(2 * CHUNKS):
        load(k).wait()
        h, c = k // CHUNKS, k % CHUNKS
        parts = parts + gram_parts(masked(x_ref[:, columns(h, c)], h, c))
    copies = share_one(0, gram_of(parts))
    for c in range(EARLY, CHUNKS - 1):
        raw_copy(c).start()
    turn = turn_one(0, copies)
    turn_out[...] = turn
    turn_copy = remote(turn_out, turn_in, turn_sem.at[0], turn_sem.at[1], partner)
    turn_copy.start()
    for c in range(max(EARLY, CHUNKS - 1), CHUNKS):
        raw_copy(c).start()

    def first_turn(which, turn_parts, block, c):
        sent0[pl.ds(2 * which, 2), :, pl.ds(c * step, step)] = turned(turn_parts, masked(block, y, c)).reshape(
            2, width, step
        )
        for side in range(2):
            for number in range(2):
                @pl.when(which == number)
                def _():
                    start_move(0, sent0, held1, number, side, c)

    own = turn_halves(turn)
    for c in range(CHUNKS):
        first_turn(y, own, x_ref[:, columns(y, c)], c)
    turn_copy.wait()
    other = turn_halves(turn_in[...])
    for c in range(CHUNKS):
        raw_copy(c).wait_recv()
        first_turn(1 - y, other, raw[:, pl.ds(c * step, step)], c)

    def plane_gram(number, held):
        parts = [jnp.zeros((full, 2 * full), jnp.float32)] * 2
        for c in range(CHUNKS):
            wait_slots(number, held, range(4), c)
            parts = [parts[which] + gram_parts(pair_block(held, which, c)) for which in range(2)]
        return [gram_of(part) for part in parts]

    for number, held, sent, held_next in ((0, held1, sent1, held2), (1, held2, sent2, held3)):
        turns = [turn_halves(t) for t in turn_two(number, plane_gram(number, held))]
        for c in range(CHUNKS):
            for which in range(2):
                sent[2 * which : 2 * which + 2, :, pl.ds(c * step, step)] = turned(
                    turns[which], pair_block(held, which, c)
                ).reshape(2, width, step)
                for side in range(2):
                    start_move(number + 1, sent, held_next, which, side, c)

    def hand_back(side, c):
        part = pl.ds(c * step, step)
        return remote(
            held3.at[2 * (1 - y) + side, :, part],
            final.at[side, :, part],
            last_send.at[side, c],
            last_recv.at[side, c],
            partner,
        )

    for c in range(CHUNKS):
        wait_slots(2, held3, (1, 2), c)
        for number in range(2):
            @pl.when(y == number)
            def _():
                hand_back(number, c).start()
    parts = [jnp.zeros((full, 2 * full), jnp.float32)] * 2
    for c in range(CHUNKS):
        wait_slots(2, held3, (0, 3), c)
        if c < LATE:
            for number in range(2):
                @pl.when(y == number)
                def _():
                    hand_back(1 - number, c).start()
        parts = [parts[which] + gram_parts(pair_block(held3, which, c)) for which in range(2)]
    mine, theirs = (jnp.where(y == k, gram_of(parts[0]), gram_of(parts[1])) for k in range(2))
    cross, tail = pack_one(theirs, width)
    singles[2, 0, pl.ds(0, width // 2)] = cross
    singles[2, 0, pl.ds(width // 2, 8)] = tail
    swap = remote(singles.at[2, 0], singles.at[2, 1], turn_sem.at[2], turn_sem.at[3], partner)
    swap.start()
    for c in range(LATE, CHUNKS):
        for number in range(2):
            @pl.when(y == number)
            def _():
                hand_back(1 - number, c).start()
    cross, tail = pack_one(mine, width)
    swap.wait()
    singles[1, r, pl.ds(0, width // 2)] = cross + singles[2, 1, pl.ds(0, width // 2)]
    singles[1, r, pl.ds(width // 2, 8)] = tail + singles[2, 1, pl.ds(width // 2, 8)]
    copies = share(singles, 1, r, rows, one_send, one_recv, lambda other: (p, other))
    own = turn_halves(turn_one(1, copies))
    for c in range(CHUNKS):
        out_ref[:, columns(y, c)] = turned(own, pair_block(held3, y, c))
    for c in range(CHUNKS):
        for side in range(2):
            hand_back(side, c).wait_recv()
        out_ref[:, columns(1 - y, c)] = turned(own, final[:, :, pl.ds(c * step, step)].reshape(full, step))

    for c in range(CHUNKS):
        raw_copy(c).wait_send()
        for which in range(2):
            for side in range(2):
                for number, sent, held in ((0, sent0, held1), (1, sent1, held2), (2, sent2, held3)):
                    end_move(number, sent, held, which, side, c)
        for side in range(2):
            hand_back(side, c).wait_send()


def solution(mesh):
    pairs, rows = mesh.shape["pair"], mesh.shape["row"]

    def body(snapshots, live_rows):
        full, cells = snapshots.shape
        width, half = full // 2, cells // 2
        state = pltpu.VMEM((4, width, half), jnp.float32)
        copies = pltpu.SemaphoreType.DMA
        return pl.pallas_call(
            functools.partial(kernel, pairs, rows),
            out_shape=jax.ShapeDtypeStruct(snapshots.shape, jnp.float32),
            in_specs=[
                pl.BlockSpec(memory_space=pltpu.SMEM),
                pl.BlockSpec(memory_space=pltpu.HBM),
            ],
            out_specs=pl.BlockSpec(memory_space=pltpu.VMEM),
            scratch_shapes=[
                pltpu.VMEM((full, cells), jnp.float32),
                pltpu.VMEM((full, half), jnp.float32),
                state,
                state,
                state,
                state,
                state,
                state,
                pltpu.VMEM((2, width, half), jnp.float32),
                pltpu.VMEM((full, full), jnp.float32),
                pltpu.VMEM((full, full), jnp.float32),
                pltpu.VMEM((3, max(rows, 2), width // 2 + 8, full), jnp.float32),
                pltpu.VMEM((2, 2 * rows, width + 8, full), jnp.float32),
                copies((2 * CHUNKS,)),
                copies((CHUNKS,)),
                copies((CHUNKS,)),
                copies((4,)),
                copies((2, rows)),
                copies((2, rows)),
                copies((2, 2 * rows)),
                copies((2, 2 * rows)),
                copies((3, 4, CHUNKS)),
                copies((3, 4, CHUNKS)),
                copies((2, CHUNKS)),
                copies((2, CHUNKS)),
            ],
            compiler_params=pltpu.CompilerParams(
                collective_id=0, has_side_effects=True, vmem_limit_bytes=48 * 1024 * 1024
            ),
        )(live_rows, snapshots)

    return jax.shard_map(
        body,
        mesh=mesh,
        in_specs=(P("pair", "row"), P("row")),
        out_specs=P("pair", "row"),
        check_vma=False,
    )
```
